32 devices in a mesh: dp: 8 (over z, x), rows: 4 (over y, core).
Axes of the slice: x: 2, y: 2, z: 4, core: 2. Of those that a mesh axis runs over, the one named last changes fastest.
Arguments:
- clean: bfloat16 [8, 32, 16, 640], P('dp', 'rows'), may hold values from -6 to 6
- noise: bfloat16 [8, 32, 16, 640], P('dp', 'rows'), may hold values from -6 to 6
- heights: int32 [8], P('dp'), may hold values from 8 to 32, as said below
- widths: int32 [8], P('dp'), may hold values from 4 to 16, as said below
- levels: int32 [8], P('dp'), may hold values from 0 to 8
- gain: float32 [640], replicated, may hold values from 0.25 to 1.75
- shift: float32 [640], replicated, may hold values from -3 to 3
- emb_table: float32 [10, 640], replicated, may hold values from -5 to 5
- w_student: bfloat16 [640, 3, 3, 640], P('dp'), may hold values from -0.078125 to 0.078125
- w_ema: bfloat16 [640, 3, 3, 640], P('dp'), may hold values from -0.078125 to 0.078125
Outputs:
- grad_conv: float32 [640, 3, 3, 640], P('dp')
- grad_gain: float32 [640], replicated
- grad_shift: float32 [640], replicated
- loss: float32 [], replicated
The draws below stay inside these ranges and needn't reach their ends.
Inputs may be any that keep to these rules, and one draw needn't show every extreme that they name: Each sample's valid rows are its first heights rows; at least one sample covers all 32 rows. Each sample's valid columns are its first widths columns; at least one sample covers all 16 columns.
All inputs are finite; a program needn't handle non-finite values.
Results may differ from the reference program's by a relative error of at most 0.00064.
Values may be sent and summed in bfloat16 or wider, within the bound.
No kernel may reach another device: no remote copies, remote signals or barrier semaphores. Data moves between devices by JAX's collectives and lax.ppermute only.
A program may use at most 128 MiB of HBM per device.

```python
import jax
import jax.numpy as jnp
from jax import lax

C = 640
GROUPS = 32
NSTEPS = 10
WID = 16
SAMPLES = 8
HGT = 32


def draw_heights(key, part):
    first_key, second_key = jax.random.split(jax.random.fold_in(key, 11))
    drawn = jax.random.randint(first_key, (SAMPLES,), HGT // 4, HGT + 1)
    chosen = jax.random.randint(second_key, (), 0, SAMPLES)
    return jnp.where(jnp.arange(SAMPLES) == chosen, HGT, drawn).astype(jnp.int32)


def draw_widths(key, part):
    first_key, second_key = jax.random.split(jax.random.fold_in(key, 23))
    drawn = jax.random.randint(first_key, (SAMPLES,), WID // 4, WID + 1)
    chosen = jax.random.randint(second_key, (), 0, SAMPLES)
    return jnp.where(jnp.arange(SAMPLES) == chosen, WID, drawn).astype(jnp.int32)


def plant(values, rng, smallest, high):
    extent = values.shape
    place = [jax.random.randint(jax.random.fold_in(rng, axis), (), 0, extent[axis]) for axis in range(len(extent))]
    values = values.at[tuple(place)].set(smallest)
    longest = extent.index(max(extent))
    place[longest] = (place[longest] + 1) % extent[longest]
    return values.at[tuple(place)].set(high)


def steps_of(key, extent, pieces, smallest, top_value):
    loudness, own = 1.0, jax.random.fold_in(key, 6)
    for dim, parts in pieces:
        steps = jnp.exp(jax.random.uniform(jax.random.fold_in(own, dim), (parts,), jnp.float32, smallest / len(pieces), top_value / len(pieces)))
        loudness = loudness * jnp.repeat(steps, extent[dim] // parts).reshape([-1 if axis == dim else 1 for axis in range(len(extent))])
    return loudness


def scatter_about(own_key, shape, scale, limit, shards=(), held_as=jnp.bfloat16):
    entries = scale * jax.random.normal(own_key, shape, jnp.float32)
    if shards:
        entries = entries * steps_of(own_key, shape, shards, -0.22, 0.18)
    return jnp.clip(entries, -limit, limit).astype(held_as)


def setup_inputs(seed: int = 0) -> dict:
    seeds = jax.random.split(jax.random.key(seed), 11)
    return {
        "clean": scatter_about(seeds[0], (SAMPLES, HGT, WID, C), 1.0, 6.0, ((0, 8), (1, 4))),
        "noise": scatter_about(seeds[1], (SAMPLES, HGT, WID, C), 1.0, 6.0, ((0, 8), (1, 4))),
        "heights": draw_heights(jax.random.fold_in(seeds[10], 71), 0),
        "widths": draw_widths(jax.random.fold_in(seeds[10], 71), 0),
        "levels": plant(jax.random.randint(seeds[4], (SAMPLES,), 0, NSTEPS - 1), jax.random.fold_in(seeds[4], 1), 0, (NSTEPS - 1) - 1).astype(jnp.int32),
        "gain": jnp.clip(1.0 + 0.15 * jax.random.normal(seeds[5], (C,), jnp.float32), 0.25, 1.75),
        "shift": scatter_about(seeds[6], (C,), 0.5, 3.0, (), jnp.float32),
        "emb_table": scatter_about(seeds[7], (NSTEPS, C), 1.0, 5.0, (), jnp.float32),
        "w_student": scatter_about(seeds[8], (C, 3, 3, C), (9 * C) ** -0.5, 0.078125, ((0, 8),)),
        "w_ema": scatter_about(seeds[9], (C, 3, 3, C), (9 * C) ** -0.5, 0.078125, ((0, 8),)),
    }


SIGMA_DATA = 0.5
SIGMA_FLOOR = 0.002
SIGMA_CEIL = 80.0

def sigma_table():
    ladder = jnp.arange(NSTEPS, dtype=jnp.float32) / (NSTEPS - 1)
    lowest = SIGMA_FLOOR ** (1.0 / 7.0)
    highest = SIGMA_CEIL ** (1.0 / 7.0)
    return (lowest + ladder * (highest - lowest)) ** 7

def scale_factors(noise_stddev):
    input_scale = 1.0 / jnp.sqrt(noise_stddev * noise_stddev + SIGMA_DATA ** 2)
    lifted = noise_stddev - SIGMA_FLOOR
    bypass_scale = SIGMA_DATA ** 2 / (lifted * lifted + SIGMA_DATA ** 2)
    output_scale = SIGMA_DATA * lifted / jnp.sqrt(SIGMA_DATA ** 2 + noise_stddev * noise_stddev)
    return (input_scale, bypass_scale, output_scale)

def silu_slope(value):
    sigmoid_value = jax.nn.sigmoid(value)
    return sigmoid_value * (1.0 + value * (1.0 - sigmoid_value))

def pad_image(image):
    return jnp.pad(image, ((1, 1), (1, 1), (0, 0)))

def conv_image(padded, weights):
    result = jnp.zeros((HGT * WID, C), jnp.float32)
    for tap_row in range(3):
        for tap_col in range(3):
            window = padded[tap_row:tap_row + HGT, tap_col:tap_col + WID, :].reshape(HGT * WID, C)
            result = result + jnp.dot(window, weights[:, tap_row, tap_col, :], preferred_element_type=jnp.float32)
    return result.reshape(HGT, WID, C)

def forward(clean_img, noise_img, valid, count, noise_stddev, embed, gain, shift, weights):
    input_scale, bypass_scale, output_scale = scale_factors(noise_stddev)
    noisy = clean_img.astype(jnp.float32) + noise_stddev * noise_img.astype(jnp.float32)
    inner = input_scale * noisy + embed
    grouped = inner.reshape(HGT, WID, GROUPS, C // GROUPS)
    weight_mask = valid[:, :, :, None]
    denom = count * (C // GROUPS)
    center = lax.optimization_barrier(jnp.sum(weight_mask * grouped, axis=(0, 1, 3))) / denom
    offset = grouped - center[:, None]
    spread = lax.optimization_barrier(jnp.sum(weight_mask * offset * offset, axis=(0, 1, 3))) / denom
    normed = ((grouped - center[:, None]) / jnp.sqrt(spread[:, None] + 1e-05)).reshape(HGT, WID, C)
    preact = normed * gain + shift
    active = (valid * jax.nn.silu(preact)).astype(jnp.bfloat16)
    padded = pad_image(active)
    conv_out = conv_image(padded, weights)
    output = bypass_scale * noisy + output_scale * (input_scale * noisy + conv_out)
    return (output, padded, normed, preact)

def reference(clean, noise, heights, widths, levels, gain, shift, emb_table, w_student, w_ema):
    noise_stddevs = sigma_table()
    rows_at = jnp.arange(HGT, dtype=jnp.int32)[:, None, None]
    cols_at = jnp.arange(WID, dtype=jnp.int32)[None, :, None]

    def one_sample(carry, items):
        clean_img, noise_img, height, width, noise_level = items
        valid = ((rows_at < height) & (cols_at < width)).astype(jnp.float32)
        count = (height * width).astype(jnp.float32)
        target, _, _, _ = forward(clean_img, noise_img, valid, count, noise_stddevs[noise_level], emb_table[noise_level], gain, shift, w_ema)
        student, padded, normed, preact = forward(clean_img, noise_img, valid, count, noise_stddevs[noise_level + 1], emb_table[noise_level + 1], gain, shift, w_student)
        delta = valid * (student - target)
        loss_term = jnp.sum(delta * delta) / count
        output_scale = scale_factors(noise_stddevs[noise_level + 1])[2]
        grad_out = (2.0 * output_scale / count * delta).astype(jnp.bfloat16)
        grad_flat = grad_out.reshape(HGT * WID, C)
        tap_rows = []
        for tap_row in range(3):
            tap_list = []
            for tap_col in range(3):
                window = padded[tap_row:tap_row + HGT, tap_col:tap_col + WID, :].reshape(HGT * WID, C)
                tap_list.append(jnp.dot(window.T, grad_flat, preferred_element_type=jnp.float32))
            tap_rows.append(jnp.stack(tap_list, 1))
        weight_grad = jnp.stack(tap_rows, 1)
        grad_pad = pad_image(grad_out)
        back = jnp.zeros((HGT * WID, C), jnp.float32)
        for tap_row in range(3):
            for tap_col in range(3):
                window = grad_pad[2 - tap_row:2 - tap_row + HGT, 2 - tap_col:2 - tap_col + WID, :].reshape(HGT * WID, C)
                back = back + jnp.dot(window, w_student[:, tap_row, tap_col, :].T, preferred_element_type=jnp.float32)
        back = back.reshape(HGT, WID, C)
        grad_pre = back * valid * silu_slope(preact)
        updated = (carry[0] + weight_grad, carry[1] + lax.optimization_barrier(jnp.sum(grad_pre * normed, axis=(0, 1))), carry[2] + lax.optimization_barrier(jnp.sum(grad_pre, axis=(0, 1))), carry[3] + loss_term)
        return (updated, None)
    start = (jnp.zeros((C, 3, 3, C), jnp.float32), jnp.zeros((C,), jnp.float32), jnp.zeros((C,), jnp.float32), jnp.zeros((), jnp.float32))
    final, _ = lax.scan(one_sample, start, (clean, noise, heights, widths, levels))
    return (final[0], final[1], final[2], final[3] / (SAMPLES * C))
```

```python
import jax
import jax.numpy as jnp
from jax import lax
from jax.sharding import PartitionSpec as P

GROUP_WIDTH = 20
NSTEPS = 10
SIGMA_DATA = 0.5
SIGMA_FLOOR = 0.002
SIGMA_CEIL = 80.0
EPS = 1e-05


def sigma_table():
    ladder = jnp.arange(NSTEPS, dtype=jnp.float32) / (NSTEPS - 1)
    lowest = SIGMA_FLOOR ** (1.0 / 7.0)
    highest = SIGMA_CEIL ** (1.0 / 7.0)
    return (lowest + ladder * (highest - lowest)) ** 7


def scale_factors(noise_stddev):
    input_scale = 1.0 / jnp.sqrt(noise_stddev * noise_stddev + SIGMA_DATA**2)
    lifted = noise_stddev - SIGMA_FLOOR
    bypass_scale = SIGMA_DATA**2 / (lifted * lifted + SIGMA_DATA**2)
    output_scale = SIGMA_DATA * lifted / jnp.sqrt(SIGMA_DATA**2 + noise_stddev * noise_stddev)
    return (input_scale, bypass_scale, output_scale)


def xor_perm(count, step):
    return [(i, i ^ step) for i in range(count)]


def rows_halo(low_row, high_row):
    count = lax.axis_size("rows")
    forward = [(i, i + 1) for i in range(count - 1)]
    backward = [(i + 1, i) for i in range(count - 1)]
    return lax.ppermute(high_row, "rows", forward), lax.ppermute(low_row, "rows", backward)


def swap_weights(own):
    dp, rows = lax.axis_size("dp"), lax.axis_size("rows")
    taps = own.shape[0]
    share = -(-taps // rows)
    r = lax.axis_index("rows")
    full = jnp.pad(own, ((0, share * rows - taps), (0, 0), (0, 0)))
    piece = lax.dynamic_slice_in_dim(full, r * share, share, 0)
    held = lax.ppermute(piece, "dp", xor_perm(dp, 1))[None]
    step = rows // 2
    while step >= 1:
        held = jnp.concatenate([held, lax.ppermute(held, "rows", xor_perm(rows, step))], 0)
        step //= 2
    bits = rows.bit_length() - 1
    out = jnp.zeros((rows,) + piece.shape, piece.dtype)
    for p in range(rows):
        code = 0
        for b in range(bits):
            if p >> b & 1:
                code |= rows >> (b + 1)
        out = lax.dynamic_update_slice_in_dim(out, held[p][None], r ^ code, 0)
    return out.reshape((rows * share,) + piece.shape[1:])[:taps]


def share_sum_rows(part):
    rows = lax.axis_size("rows")
    r = lax.axis_index("rows")
    half = part.shape[0] // 2
    low = (r & 1) == 0
    mine = jnp.where(low, part[:half], part[half:])
    other = jnp.where(low, part[half:], part[:half])
    mine = mine + lax.ppermute(other, "rows", xor_perm(rows, 1))
    step = 2
    while step < rows:
        mine = mine + lax.ppermute(mine, "rows", xor_perm(rows, step))
        step *= 2
    got = lax.ppermute(mine, "rows", xor_perm(rows, 1))
    return jnp.concatenate([jnp.where(low, mine, got), jnp.where(low, got, mine)], 0)


def butterfly(value):
    for axis in ("rows", "dp"):
        count = lax.axis_size(axis)
        step = 1
        while step < count:
            value = value + lax.ppermute(value, axis, xor_perm(count, step))
            step *= 2
    return value


def shards(clean, noise, heights, widths, levels, gain, shift, emb_table, w_student, w_ema):
    f32, bf16 = jnp.float32, jnp.bfloat16
    dp, rows = lax.axis_size("dp"), lax.axis_size("rows")
    nz = dp // 2
    channels = clean.shape[3]
    hr, wid = clean.shape[1], clean.shape[2]
    px = hr * wid
    cd = channels // dp
    cg = 2 * cd
    ng = cg // GROUP_WIDTH
    k = lax.axis_index("dp")
    m, zi = k % 2, k // 2
    r = lax.axis_index("rows")

    own_s = w_student.transpose(1, 2, 0, 3).reshape(9, cd, channels)
    own_t = w_ema.transpose(1, 2, 0, 3).reshape(9, cd, channels)
    own_w = jnp.concatenate([own_s, own_t], 0)
    nbr_w = swap_weights(own_w)
    full_w = jnp.concatenate([own_w, nbr_w], 1)
    wg_s = full_w[:9].reshape(3, 3, cg, channels)
    wg_t = full_w[9:].reshape(3, 3, cg, channels)

    both = jnp.concatenate([clean.reshape(px, channels), noise.reshape(px, channels)], 0)
    split = both.reshape(2 * px, nz, 2, cd)
    split = jnp.where(m == 0, split, split[:, :, ::-1, :])
    split = split.reshape(2 * px, nz, cg).transpose(1, 0, 2)
    facts = jnp.stack([heights[0], widths[0], levels[0]]).astype(bf16)
    facts = jnp.pad(facts[None, :], ((0, 15), (0, cg - 3)))
    split = jnp.concatenate([split, jnp.broadcast_to(facts, (nz,) + facts.shape)], 1)
    order = [0] + list(range(nz - 1, 0, -1))
    got = {}
    for s in order:
        piece = lax.dynamic_index_in_dim(split, zi ^ s, 0, keepdims=False)
        got[s] = piece if s == 0 else lax.ppermute(piece, "dp", xor_perm(dp, 2 * s))
    held = jnp.stack([got[s] for s in range(nz)], 0)
    cn = held[:, : 2 * px].reshape(nz, 2, hr, wid, cg)
    facts = held[:, 2 * px, :3].astype(f32)
    height, width, level = facts[:, 0], facts[:, 1], facts[:, 2]
    above, below = rows_halo(cn[:, :, :1], cn[:, :, -1:])

    table = sigma_table()
    ids = jnp.arange(NSTEPS, dtype=f32)[None, :]
    count = height * width
    rel = jnp.arange(2)
    pair_gain = jnp.concatenate([lax.dynamic_slice_in_dim(gain, (k ^ j) * cd, cd, 0) for j in range(2)])
    pair_shift = jnp.concatenate([lax.dynamic_slice_in_dim(shift, (k ^ j) * cd, cd, 0) for j in range(2)])
    pair_emb = jnp.concatenate(
        [lax.dynamic_slice_in_dim(emb_table, (k ^ j) * cd, cd, 1) for j in range(2)], 1
    )
    rows_at = r * hr - 1 + jnp.arange(hr + 2, dtype=jnp.int32)
    rows_at = rows_at.astype(f32)
    cols_at = jnp.arange(wid, dtype=f32)
    valid = (
        (rows_at[None, :, None] >= 0)
        & (rows_at[None, :, None] < height[:, None, None])
        & (cols_at[None, None, :] < width[:, None, None])
    ).astype(f32)[..., None]
    inside = valid[:, 1:-1]
    starts = (jnp.arange(rows, dtype=f32) * hr)[:, None]
    block_count = jnp.clip(height[None, :] - starts, 0, hr) * width[None, :]
    own_count = lax.dynamic_index_in_dim(block_count, r, 0, keepdims=False)

    def pass_scalars(level_id):
        hot = (level_id[:, None] == ids).astype(f32)
        sigma = jnp.sum(hot * table[None, :], 1)
        emb = jnp.sum(hot[:, :, None] * pair_emb[None], 1)
        return sigma, emb

    def inner_of(block, sigma, emb):
        in_scale = scale_factors(sigma)[0][:, None, None, None]
        noisy = block[:, 0].astype(f32) + sigma[:, None, None, None] * block[:, 1].astype(f32)
        return in_scale * noisy + emb[:, None, None, :]

    spread_to = jnp.repeat(jnp.eye(ng, dtype=f32), GROUP_WIDTH, axis=1)

    def to_groups(per_channel):
        return per_channel.reshape(nz, ng, GROUP_WIDTH).sum(2)

    def to_channels(per_group):
        return jnp.repeat(per_group, GROUP_WIDTH, axis=1)

    passes = [pass_scalars(level), pass_scalars(level + 1.0)]
    safe = jnp.maximum(own_count * GROUP_WIDTH, 1.0)[:, None]
    local = []
    for sigma, emb in passes:
        inner = inner_of(cn, sigma, emb)
        mean = to_groups(jnp.sum(inside * inner, (1, 2))) / safe
        off = inner - to_channels(mean)[:, None, None, :]
        local += [mean, to_groups(jnp.sum(inside * off * off, (1, 2)))]
    local = jnp.stack(local, 0).reshape(4 * nz, ng)
    stats = [local] + [lax.ppermute(local, "rows", xor_perm(rows, s)) for s in range(1, rows)]
    stats = jnp.stack(stats, 0).reshape(rows, 2, 2, nz, ng)
    counts = jnp.stack([lax.dynamic_index_in_dim(block_count, r ^ s, 0, keepdims=False) for s in range(rows)])
    counts = counts[:, None, :, None]
    whole = count[None, :, None]
    center = jnp.sum(stats[:, :, 0] * counts, 0) / whole
    lift = stats[:, :, 0] - center[None]
    m2 = jnp.sum(stats[:, :, 1] + counts * GROUP_WIDTH * lift * lift, 0)
    spread = m2 / (whole * GROUP_WIDTH)

    tall = jnp.concatenate([above, cn, below], 2)

    def norm_of(block, which):
        sigma, emb = passes[which]
        inner = inner_of(block, sigma, emb)
        mid = to_channels(center[which])[:, None, None, :]
        dev = to_channels(jnp.sqrt(spread[which] + EPS))[:, None, None, :]
        return (inner - mid) / dev

    def active_of(which):
        preact = norm_of(tall, which) * pair_gain + pair_shift
        return (valid * jax.nn.silu(preact)).astype(bf16)

    act_t = active_of(0)
    act_s = active_of(1)
    dims = ("NHWC", "HWIO", "NHWC")

    def conv(act, w):
        return lax.conv_general_dilated(
            act, w, (1, 1), ((0, 0), (1, 1)), dimension_numbers=dims, preferred_element_type=f32
        )

    out_t = scale_factors(passes[0][0])[2]
    out_s = scale_factors(passes[1][0])[2]
    part = out_s[:, None, None, None] * conv(act_s, wg_s) - out_t[:, None, None, None] * conv(act_t, wg_t)
    act_x = lax.ppermute(act_s[..., cd:], "dp", xor_perm(dp, 1))
    total = part[0]
    for s in range(nz - 1, 0, -1):
        total = total + lax.ppermute(part[s], "dp", xor_perm(dp, 2 * s))

    def own_terms(which):
        sigma = passes[which][0][0]
        in_scale, bypass, out_scale = scale_factors(sigma)
        noisy = clean[0].astype(f32) + sigma * noise[0].astype(f32)
        return bypass * noisy + out_scale * (in_scale * noisy)

    delta = inside[0] * (own_terms(1) - own_terms(0) + total)
    loss_local = jnp.sum(delta * delta) / count[0]
    grad = (2.0 * out_s[0] / count[0] * delta).astype(bf16)
    grads = {0: grad}
    for s in range(nz - 1, 0, -1):
        grads[s] = lax.ppermute(grad, "dp", xor_perm(dp, 2 * s))
    grads_x = [lax.ppermute(grads[s], "dp", xor_perm(dp, 1)) for s in range(nz)]
    grad_z = jnp.stack([grads[s] for s in range(nz)], 0)
    grad_x = jnp.stack(grads_x, 0)

    g_above, g_below = rows_halo(grad_z[:, :1], grad_z[:, -1:])
    grad_tall = jnp.concatenate([g_above, grad_z, g_below], 1)
    back = lax.conv_general_dilated(
        grad_tall,
        wg_s[::-1, ::-1],
        (1, 1),
        ((0, 0), (1, 1)),
        dimension_numbers=("NHWC", "HWOI", "NHWC"),
        preferred_element_type=f32,
    )
    normed = norm_of(cn, 1)
    preact = normed * pair_gain + pair_shift
    gate = jax.nn.sigmoid(preact)
    grad_pre = back * inside * (gate * (1.0 + preact * (1.0 - gate)))
    small = jnp.stack([jnp.sum(grad_pre * normed, (0, 1, 2)), jnp.sum(grad_pre, (0, 1, 2))], 0)
    placed = jnp.zeros((2, dp, cd), f32)
    for j in range(2):
        placed = lax.dynamic_update_slice(
            placed, small[:, None, j * cd : (j + 1) * cd], (0, k ^ j, 0)
        )
    flat = jnp.concatenate([placed.reshape(2 * channels), loss_local[None]])
    flat = jnp.pad(flat, (0, -flat.shape[0] % 1024)).reshape(-1, 128)
    flat = butterfly(flat).reshape(-1)

    def windows(act):
        wide = jnp.pad(act, ((0, 0), (0, 0), (1, 1), (0, 0)))
        return [wide[:, i : i + hr, j : j + wid].reshape(nz * px, cd) for i in range(3) for j in range(3)]

    left = jnp.concatenate(
        [jnp.concatenate(windows(act_s[..., :cd]), 1), jnp.concatenate(windows(act_x), 1)], 0
    )
    right = jnp.concatenate([grad_z.reshape(nz * px, channels), grad_x.reshape(nz * px, channels)], 0)
    owned = lax.dot_general(left, right, (((0,), (0,)), ((), ())), preferred_element_type=f32)
    grad_conv = share_sum_rows(owned).reshape(3, 3, cd, channels).transpose(2, 0, 1, 3)
    loss = flat[2 * channels] / (dp * channels)
    return grad_conv, flat[:channels], flat[channels : 2 * channels], loss


def solution(mesh):
    placed = (
        P("dp", "rows", None, None),
        P("dp", "rows", None, None),
        P("dp"),
        P("dp"),
        P("dp"),
        P(),
        P(),
        P(),
        P("dp", None, None, None),
        P("dp", None, None, None),
    )
    return jax.shard_map(
        shards,
        mesh=mesh,
        in_specs=placed,
        out_specs=(P("dp", None, None, None), P(), P(), P()),
        check_vma=False,
    )
```

```python
import functools

import jax
import jax.numpy as jnp
from jax import lax
from jax.experimental import pallas as pl
from jax.experimental.pallas import tpu as pltpu
from jax.sharding import PartitionSpec as P

GROUP_WIDTH = 20
NSTEPS = 10
SIGMA_DATA = 0.5
SIGMA_FLOOR = 0.002
SIGMA_CEIL = 80.0
EPS = 1e-05


f32, bf16 = jnp.float32, jnp.bfloat16


def sigma_table():
    ladder = jnp.arange(NSTEPS, dtype=f32) / (NSTEPS - 1)
    lowest = SIGMA_FLOOR ** (1.0 / 7.0)
    highest = SIGMA_CEIL ** (1.0 / 7.0)
    return (lowest + ladder * (highest - lowest)) ** 7


def scale_factors(noise_stddev):
    input_scale = 1.0 / jnp.sqrt(noise_stddev * noise_stddev + SIGMA_DATA**2)
    lifted = noise_stddev - SIGMA_FLOOR
    bypass_scale = SIGMA_DATA**2 / (lifted * lifted + SIGMA_DATA**2)
    output_scale = SIGMA_DATA * lifted / jnp.sqrt(SIGMA_DATA**2 + noise_stddev * noise_stddev)
    return (input_scale, bypass_scale, output_scale)


def xor_perm(count, step):
    return [(i, i ^ step) for i in range(count)]


def along_z(value, step):
    return lax.ppermute(value, "dp", xor_perm(lax.axis_size("dp"), 2 * step))


def along_x(value):
    return lax.ppermute(value, "dp", xor_perm(lax.axis_size("dp"), 1))


def along_rows(value, step):
    return lax.ppermute(value, "rows", xor_perm(lax.axis_size("rows"), step))


def rows_halo(low_row, high_row):
    count = lax.axis_size("rows")
    forward = [(i, i + 1) for i in range(count - 1)]
    backward = [(i + 1, i) for i in range(count - 1)]
    return lax.ppermute(high_row, "rows", forward), lax.ppermute(low_row, "rows", backward)


def swap_weights(own):
    rows = lax.axis_size("rows")
    n = own.shape[0]
    share = -(-(-(-n // rows)) // 8) * 8
    r = lax.axis_index("rows")

    def start(q):
        return jnp.minimum(q * share, n - share)

    held = [(0, along_x(lax.dynamic_slice_in_dim(own, start(r), share, 0)))]
    step = rows // 2
    while step >= 1:
        block = jnp.stack([piece for _, piece in held], 0) if len(held) > 1 else held[0][1]
        got = along_rows(block, step)
        news = [got[p] for p in range(len(held))] if len(held) > 1 else [got]
        held += [(code ^ step, piece) for (code, _), piece in zip(list(held), news)]
        step //= 2
    out = jnp.zeros_like(own)
    for code, piece in held:
        out = lax.dynamic_update_slice_in_dim(out, piece, start(r ^ code), 0)
    return out


def call(kernel, outs, *args, flops=0, smem=0, scratch=()):
    specs = [pl.BlockSpec(memory_space=pltpu.SMEM)] * smem
    specs += [pl.BlockSpec(memory_space=pltpu.VMEM)] * (len(args) - smem)
    moved = sum(a.size * a.dtype.itemsize for a in list(args) + list(outs))
    return pl.pallas_call(
        kernel,
        out_shape=outs,
        in_specs=specs,
        out_specs=[pl.BlockSpec(memory_space=pltpu.VMEM)] * len(outs),
        scratch_shapes=list(scratch),
        cost_estimate=pl.CostEstimate(flops=flops, bytes_accessed=moved, transcendentals=0),
    )(*args)


SIG, CIN, COUT, HEIGHT, WIDTH, ROW0 = 0, 2, 4, 6, 7, 8
NSCALARS = 16


def valid_mask(scalars, s, first, shape, hr, wid):
    at = lax.broadcasted_iota(jnp.int32, shape, 0)
    row = (at // wid + first).astype(f32) + scalars[s, ROW0]
    col = (at % wid).astype(f32)
    return ((row >= 0) & (row < scalars[s, HEIGHT]) & (col < scalars[s, WIDTH])).astype(f32)


def stats_kernel(hr, wid, scalars, cn, emb, out):
    nz = cn.shape[0]
    for s in range(nz):
        valid = valid_mask(scalars, s, 0, (hr * wid, cn.shape[3]), hr, wid)
        n = jnp.maximum(jnp.sum(valid[:, :1], axis=0, keepdims=True), 1.0)
        clean, noise = cn[s, 0].astype(f32), cn[s, 1].astype(f32)
        for which in range(2):
            inner = scalars[s, CIN + which] * (clean + scalars[s, SIG + which] * noise) + emb[which, s][None, :]
            mean = jnp.sum(valid * inner, axis=0, keepdims=True) / n
            off = inner - mean
            out[which, s, 0:1, :] = mean
            out[which, s, 1:2, :] = jnp.sum(valid * off * off, axis=0, keepdims=True)


def conv_kernel(samples, hr, wid, scalars, cn, above, below, emb, mid, dev, gain, shift, own_s, nbr_s, own_t, nbr_t, *refs):
    ns = len(samples)
    cg = cn.shape[3]
    cd = cg // 2
    px = hr * wid
    parts, (ja, jb, m1a, m1b, m2a, m2b, ta, tb) = refs[: 2 * ns], refs[2 * ns :]
    tall = (hr + 2) * wid
    col = lax.broadcasted_iota(jnp.int32, (tall, cg), 0) % wid
    not_first = (col > 0).astype(f32)
    not_last = (col < wid - 1).astype(f32)

    def fan(value, kind):
        left = pltpu.roll(value, 1, 0) * not_first
        right = pltpu.roll(value, tall - 1, 0) * not_last
        return [
            jnp.concatenate([v[:, h * cd : (h + 1) * cd] for v in (left, value, right)], axis=1).astype(kind)
            for h in range(2)
        ]

    for n, s in enumerate(samples):
        valid = valid_mask(scalars, s, -1, (tall, cg), hr, wid)
        blocks = [
            jnp.concatenate([above[s, p].astype(f32), cn[s, p].astype(f32), below[s, p].astype(f32)], axis=0)
            for p in range(2)
        ]
        for which in range(2):
            noisy = blocks[0] + scalars[s, SIG + which] * blocks[1]
            inner = scalars[s, CIN + which] * noisy + emb[which, s][None, :]
            normed = (inner - mid[which, s][None, :]) * dev[which, s][None, :]
            preact = normed * gain[0][None, :] + shift[0][None, :]
            gate = 1.0 / (1.0 + jnp.exp(-preact))
            active = valid * (preact * gate)
            if which == 0:
                ta[n], tb[n] = fan(active, bf16)
            else:
                ja[n], jb[n] = fan(active, bf16)
                slope = valid * (gate * (1.0 + preact * (1.0 - gate)))
                m2a[n], m2b[n] = fan(slope, f32)
                m1a[n], m1b[n] = fan(slope * normed, f32)

    def conv(a, b, wa, wb):
        total = None
        for i in range(3):
            for j, w in ((a, wa), (b, wb)):
                left = j[:, i * wid : i * wid + px, :].reshape(ns * px, 3 * cd)
                term = jnp.dot(left, w[i], preferred_element_type=f32)
                total = term if total is None else total + term
        return total.reshape(ns, px, -1)

    student = conv(ja, jb, own_s, nbr_s)
    target = conv(ta, tb, own_t, nbr_t)
    half = px // 2
    for n, s in enumerate(samples):
        part = scalars[s, COUT + 1] * student[n] - scalars[s, COUT] * target[n]
        parts[2 * n][...] = part[:half]
        parts[2 * n + 1][...] = part[half:]


def sums_kernel(wid, grads, own, nbr, m1a, m1b, m2a, m2b, out):
    nz, px, o = grads.shape
    left = grads[...].reshape(nz * px, o)
    for h, (w, m1, m2) in enumerate(((own, m1a, m2a), (nbr, m1b, m2b))):
        for row in range(2):
            out[2 * h + row] = jnp.zeros(out.shape[1:], f32)
        for i in range(3):
            seen = lax.dot_general(left, w[i], (((1,), (1,)), ((), ())), preferred_element_type=f32)
            for row, mm in enumerate((m1, m2)):
                field = mm[:, i * wid : i * wid + px, :].reshape(nz * px, -1)
                out[2 * h + row, 0:1, :] += jnp.sum(seen * field, axis=0, keepdims=True)


def grad_kernel(wid, j, grads, out):
    nz, px, o = grads.shape
    right = grads[...].reshape(nz * px, o)
    for i in range(3):
        left = j[:, i * wid : i * wid + px, :].reshape(nz * px, -1)
        out[i] = lax.dot_general(left, right, (((0,), (0,)), ((), ())), preferred_element_type=f32)


def grad_add_kernel(wid, j, grads, before, out):
    nz, px, o = grads.shape
    right = grads[...].reshape(nz * px, o)
    for i in range(3):
        left = j[:, i * wid : i * wid + px, :].reshape(nz * px, -1)
        out[i] = before[i] + lax.dot_general(left, right, (((0,), (0,)), ((), ())), preferred_element_type=f32)


def small_sum(value):
    rows, dp = lax.axis_size("rows"), lax.axis_size("dp")
    for axis, count, base in (("rows", rows, 1), ("dp", 2, 1), ("dp", dp // 2, 2)):
        step = 1
        while step < count:
            value = value + lax.ppermute(value, axis, xor_perm(lax.axis_size(axis), step * base))
            step *= 2
    return value


def shards(clean, noise, heights, widths, levels, gain, shift, emb_table, w_student, w_ema):
    dp, rows = lax.axis_size("dp"), lax.axis_size("rows")
    nz = dp // 2
    channels = clean.shape[3]
    hr, wid = clean.shape[1], clean.shape[2]
    px = hr * wid
    cd = channels // dp
    cg = 2 * cd
    ng = cg // GROUP_WIDTH
    k = lax.axis_index("dp")
    m, zi = k % 2, k // 2
    r = lax.axis_index("rows")

    both = jnp.concatenate([clean.reshape(px, channels), noise.reshape(px, channels)], 0)
    split = both.reshape(2 * px, nz, 2, cd)
    split = jnp.where(m == 0, split, split[:, :, ::-1, :])
    split = split.reshape(2 * px, nz, cg).transpose(1, 0, 2)
    facts = jnp.stack([heights[0], widths[0], levels[0]]).astype(bf16)
    facts = jnp.pad(facts[None, :], ((0, 15), (0, cg - 3)))
    split = jnp.concatenate([split, jnp.broadcast_to(facts, (nz,) + facts.shape)], 1)
    split, w_student, w_ema = lax.optimization_barrier((split, w_student, w_ema))
    got = {0: lax.dynamic_index_in_dim(split, zi, 0, keepdims=False)}
    for s in range(nz - 1, 0, -1):
        got[s] = along_z(lax.dynamic_index_in_dim(split, zi ^ s, 0, keepdims=False), s)

    own_s = w_student.transpose(1, 2, 0, 3).reshape(9 * cd, channels)
    own_t = w_ema.transpose(1, 2, 0, 3).reshape(9 * cd, channels)
    nbr_s, nbr_t = swap_weights(own_s), swap_weights(own_t)
    own_s, own_t, nbr_s, nbr_t = (w.reshape(3, 3 * cd, channels) for w in (own_s, own_t, nbr_s, nbr_t))

    held = jnp.stack([got[s] for s in range(nz)], 0)
    cn = held[:, : 2 * px].reshape(nz, 2, px, cg)
    above, below = rows_halo(cn[:, :, :wid], cn[:, :, px - wid :])
    facts = held[:, 2 * px, :3].astype(f32)
    height, width, level = facts[:, 0], facts[:, 1], facts[:, 2]

    ids = jnp.arange(NSTEPS, dtype=f32)
    count = height * width
    pair_gain = jnp.concatenate([lax.dynamic_slice_in_dim(gain, (k ^ j) * cd, cd, 0) for j in range(2)])
    pair_shift = jnp.concatenate([lax.dynamic_slice_in_dim(shift, (k ^ j) * cd, cd, 0) for j in range(2)])
    pair_emb = jnp.concatenate([lax.dynamic_slice_in_dim(emb_table, (k ^ j) * cd, cd, 1) for j in range(2)], 1)
    level2 = jnp.stack([level, level + 1.0], 0)
    hot = (level2[:, :, None] == ids).astype(f32)
    sigma = jnp.sum(hot * sigma_table(), 2)
    emb = jnp.sum(hot[..., None] * pair_emb, 2)
    in_scale, bypass, out_scale = scale_factors(sigma)
    row0 = jnp.full((1, nz), r * hr, f32)
    scalars = jnp.concatenate([sigma, in_scale, out_scale, height[None], width[None], row0], 0).T
    scalars = jnp.pad(scalars, ((0, 0), (0, NSCALARS - scalars.shape[1])))

    sds = jax.ShapeDtypeStruct
    (local,) = call(
        functools.partial(stats_kernel, hr, wid), [sds((2, nz, 2, cg), f32)], scalars, cn, emb, smem=1
    )
    stats = jnp.stack([local] + [along_rows(local, s) for s in range(1, rows)], 0)
    starts = jnp.stack([(r ^ s) * hr for s in range(rows)]).astype(f32)[:, None]
    counts = (jnp.clip(height[None, :] - starts, 0, hr) * width[None, :])[:, None, :, None]

    def group_total(per_channel):
        summed = per_channel.reshape(2, nz, ng, GROUP_WIDTH).sum(3) / (count * GROUP_WIDTH)[None, :, None]
        return jnp.repeat(summed, GROUP_WIDTH, axis=2)

    center = group_total(jnp.sum(stats[:, :, :, 0] * counts, 0))
    lift = stats[:, :, :, 0] - center[None]
    spread = group_total(jnp.sum(stats[:, :, :, 1] + counts * lift * lift, 0))
    dev = 1.0 / jnp.sqrt(spread + EPS)

    tall = (hr + 2) * wid
    part, fans = {}, {}
    for first in (1, 0):
        samples = tuple(range(first, nz, 2))
        ns = len(samples)
        outs = [sds((px // 2, channels), f32)] * (2 * ns)
        outs += [sds((ns, tall, 3 * cd), bf16)] * 2 + [sds((ns, tall, 3 * cd), f32)] * 4
        res = call(
            functools.partial(conv_kernel, samples, hr, wid),
            outs, scalars, cn, above, below, emb, center, dev, pair_gain[None], pair_shift[None],
            own_s, nbr_s, own_t, nbr_t,
            smem=1, flops=4 * ns * px * 9 * cg * channels,
            scratch=[pltpu.VMEM((ns, tall, 3 * cd), bf16)] * 2,
        )
        for n, s in enumerate(samples):
            part[s] = [res[2 * n], res[2 * n + 1]]
        fans[first] = res[2 * ns :]

    def merged(at):
        rest = fans[0][at].shape[1:]
        return jnp.stack([fans[0][at], fans[1][at]], 1).reshape((nz,) + rest)

    j_own, j_nbr, m1a, m1b, m2a, m2b = (merged(at) for at in range(6))

    bit = 1
    while bit < nz:
        for s in range(nz - 1, -1, -1):
            if s % (2 * bit) == 0:
                part[s] = [part[s][h] + along_z(part[s ^ bit][h], bit) for h in range(2)]
        bit *= 2
    total = jnp.concatenate(part[0], 0)
    j_x = along_x(j_nbr)

    own_clean, own_noise = clean.reshape(px, channels).astype(f32), noise.reshape(px, channels).astype(f32)

    def own_terms(which):
        noisy = own_clean + sigma[which, 0] * own_noise
        return bypass[which, 0] * noisy + out_scale[which, 0] * (in_scale[which, 0] * noisy)

    at = jnp.arange(px, dtype=jnp.int32)
    inside = (((at // wid + r * hr).astype(f32) < height[0]) & ((at % wid).astype(f32) < width[0])).astype(f32)
    delta = inside[:, None] * (own_terms(1) - own_terms(0) + total)
    loss_local = jnp.sum(delta * delta) / count[0]
    grad = (2.0 * out_scale[1, 0] / count[0] * delta).astype(bf16)
    grads = {0: grad}
    bit = nz // 2
    while bit >= 1:
        for s in sorted(grads):
            grads[s ^ bit] = along_z(grads[s], bit)
        bit //= 2
    grad_x = jnp.stack([along_x(grads[s]) for s in range(nz)], 0)
    grad_z = jnp.stack([grads[s] for s in range(nz)], 0)

    work = 2 * nz * px * 9 * cd * channels
    (small,) = call(
        functools.partial(sums_kernel, wid),
        [sds((4, 8, 3 * cd), f32)],
        grad_z, own_s, nbr_s, m1a, m1b, m2a, m2b,
        flops=2 * work,
    )
    small = small[:, 0].reshape(2, 2, 3, cd).sum(2)
    placed = jnp.zeros((2, dp, cd), f32)
    for h in range(2):
        placed = lax.dynamic_update_slice(placed, small[h][:, None, :], (0, k ^ h, 0))
    flat = jnp.concatenate([placed.reshape(2 * channels), loss_local[None]])
    flat = jnp.pad(flat, (0, -flat.shape[0] % 1024)).reshape(-1, 128)
    flat = small_sum(flat)

    shape = sds((3, 3 * cd, channels), f32)
    (owned,) = call(functools.partial(grad_kernel, wid), [shape], j_own, grad_z, flops=work)
    (owned,) = call(functools.partial(grad_add_kernel, wid), [shape], j_x, grad_x, owned, flops=work)
    owned = owned.reshape(9 * cd, channels)
    half = 9 * cd // 2
    low = (r & 1) == 0
    mine = jnp.where(low, owned[:half], owned[half:])
    other = jnp.where(low, owned[half:], owned[:half])
    mine = mine + along_rows(other, 1)
    step = 2
    while step < rows:
        came = along_rows(mine, step)
        if step == 2:
            mine, flat = lax.optimization_barrier((mine, flat))
        mine = mine + came
        step *= 2
    back = along_rows(mine, 1)
    owned = jnp.concatenate([jnp.where(low, mine, back), jnp.where(low, back, mine)], 0)
    grad_conv = owned.reshape(3, 3, cd, channels).transpose(2, 0, 1, 3)
    flat = flat.reshape(-1)
    loss = flat[2 * channels] / (dp * channels)
    return grad_conv, flat[:channels], flat[channels : 2 * channels], loss


def solution(mesh):
    placed = (
        P("dp", "rows", None, None),
        P("dp", "rows", None, None),
        P("dp"),
        P("dp"),
        P("dp"),
        P(),
        P(),
        P(),
        P("dp", None, None, None),
        P("dp", None, None, None),
    )
    return jax.shard_map(
        shards,
        mesh=mesh,
        in_specs=placed,
        out_specs=(P("dp", None, None, None), P(), P(), P()),
        check_vma=False,
    )
```

```python
import functools

import jax
import jax.numpy as jnp
from jax import lax
from jax.experimental import pallas as pl
from jax.experimental.pallas import tpu as pltpu
from jax.sharding import PartitionSpec as P

GROUP_WIDTH = 20
NSTEPS = 10
SIGMA_DATA = 0.5
SIGMA_FLOOR = 0.002
SIGMA_CEIL = 80.0
EPS = 1e-05


f32, bf16 = jnp.float32, jnp.bfloat16


def sigma_table():
    ladder = jnp.arange(NSTEPS, dtype=f32) / (NSTEPS - 1)
    lowest = SIGMA_FLOOR ** (1.0 / 7.0)
    highest = SIGMA_CEIL ** (1.0 / 7.0)
    return (lowest + ladder * (highest - lowest)) ** 7


def scale_factors(noise_stddev):
    input_scale = 1.0 / jnp.sqrt(noise_stddev * noise_stddev + SIGMA_DATA**2)
    lifted = noise_stddev - SIGMA_FLOOR
    bypass_scale = SIGMA_DATA**2 / (lifted * lifted + SIGMA_DATA**2)
    output_scale = SIGMA_DATA * lifted / jnp.sqrt(SIGMA_DATA**2 + noise_stddev * noise_stddev)
    return (input_scale, bypass_scale, output_scale)


def xor_perm(count, step):
    return [(i, i ^ step) for i in range(count)]


def along_z(value, step):
    return lax.ppermute(value, "dp", xor_perm(lax.axis_size("dp"), 2 * step))


def along_x(value):
    return lax.ppermute(value, "dp", xor_perm(lax.axis_size("dp"), 1))


def along_rows(value, step):
    return lax.ppermute(value, "rows", xor_perm(lax.axis_size("rows"), step))


def rows_halo(low_row, high_row):
    count = lax.axis_size("rows")
    forward = [(i, i + 1) for i in range(count - 1)]
    backward = [(i + 1, i) for i in range(count - 1)]
    return lax.ppermute(high_row, "rows", forward), lax.ppermute(low_row, "rows", backward)


ANY = pl.BlockSpec(memory_space=pl.ANY)
SMEM = pl.BlockSpec(memory_space=pltpu.SMEM)
VMEM = pl.BlockSpec(memory_space=pltpu.VMEM)
sds = jax.ShapeDtypeStruct


def call(kernel, outs, args, specs=None, flops=0, scratch=()):
    specs = specs or {}
    moved = sum(a.size * a.dtype.itemsize for n, a in enumerate(args) if specs.get(n) is not ANY)
    moved += sum(a.size * a.dtype.itemsize for a in outs)
    res = pl.pallas_call(
        kernel,
        out_shape=outs,
        in_specs=[specs.get(n, VMEM) for n in range(len(args))],
        out_specs=[VMEM] * len(outs),
        scratch_shapes=list(scratch),
        cost_estimate=pl.CostEstimate(flops=flops, bytes_accessed=moved, transcendentals=0),
    )(*args)
    return list(res)


SIG, CIN, COUT, BYP, HEIGHT, WIDTH = range(6)


def payload_kernel(nz, cd, facts, clean, noise, *outs):
    px, channels = clean.shape
    cg = 2 * cd
    source = lax.broadcasted_iota(jnp.int32, (channels, cg), 0)
    at = lax.broadcasted_iota(jnp.int32, (channels, cg), 1)
    lane = lax.broadcasted_iota(jnp.int32, (16, cg), 1)
    row = jnp.where(lane == 0, facts[0], jnp.where(lane == 1, facts[1], jnp.where(lane == 2, facts[2], 0)))
    for s in range(nz):
        base = ((facts[3] // 2) ^ s) * cg
        own, nbr = base + (facts[3] % 2) * cd, base + (1 - facts[3] % 2) * cd
        pick = (source == jnp.where(at < cd, own + at, nbr + at - cd)).astype(f32).astype(bf16)
        outs[s][:px] = jnp.dot(clean[...], pick, preferred_element_type=f32).astype(bf16)
        outs[s][px : 2 * px] = jnp.dot(noise[...], pick, preferred_element_type=f32).astype(bf16)
        outs[s][2 * px :] = row.astype(f32).astype(bf16)


def share_kernel(start, own_s, own_t, after, out_s, out_t, sems):
    size = out_s.shape[0]
    at = pl.multiple_of(start[0], 16)
    copies = [
        pltpu.make_async_copy(w.at[pl.ds(at, size)], out, sems.at[n])
        for n, (w, out) in enumerate(((own_s, out_s), (own_t, out_t)))
    ]
    for copy in copies:
        copy.start()
    for copy in copies:
        copy.wait()


def place_kernel(starts, *refs):
    pieces, out = refs[:-1], refs[-1]
    for n, piece in enumerate(pieces):
        out[pl.ds(pl.multiple_of(starts[n], 16), piece.shape[0]), :] = piece[...]


def swap_weights(own_s, own_t, after):
    rows = lax.axis_size("rows")
    n = own_s.shape[0]
    share = -(-(-(-n // rows)) // 16) * 16
    r = lax.axis_index("rows")

    def start(q):
        return jnp.minimum(q * share, n - share)

    if n % 16:
        shares = [lax.dynamic_slice_in_dim(w, start(r), share, 0) for w in (own_s, own_t)]
    else:
        out = sds((share, own_s.shape[1]), bf16)
        shares = call(
            share_kernel, [out, out], [start(r)[None], own_s, own_t, after],
            {0: SMEM, 1: ANY, 2: ANY, 3: ANY}, scratch=[pltpu.SemaphoreType.DMA((2,))],
        )
    results = []
    for name, cut, own in zip("st", shares, (own_s, own_t)):
        with jax.named_scope("w_x_" + name):
            held = [(0, along_x(cut))]
        step = rows // 2
        while step >= 1:
            with jax.named_scope("w_rows_" + name):
                held += [(code ^ step, along_rows(piece, step)) for code, piece in list(held)]
            step //= 2
        starts = jnp.stack([start(r ^ code) for code, _ in held])
        if n % 16:
            out = jnp.zeros_like(own)
            for p, (_, piece) in enumerate(held):
                out = lax.dynamic_update_slice_in_dim(out, piece, starts[p], 0)
        else:
            (out,) = call(
                place_kernel, [sds(own.shape, bf16)], [starts] + [piece for _, piece in held], {0: SMEM}
            )
        results.append(out)
    return results


def spot(rows, at, column):
    return rows[at : at + 1, column : column + 1]


def valid_mask(facts, at, row0, first, shape, hr, wid):
    pixel = lax.broadcasted_iota(jnp.int32, shape, 0)
    row = (pixel // wid + (first + row0)).astype(f32)
    col = (pixel % wid).astype(f32)
    return ((row >= 0) & (row < spot(facts, at, HEIGHT)) & (col < spot(facts, at, WIDTH))).astype(f32)


def stats_kernel(nz, hr, wid, row0, table, emb_pair, *refs):
    blocks, (facts, emb, local, low, high) = refs[:nz], refs[nz:]
    px = hr * wid
    cg = emb.shape[1]
    lane = lax.broadcasted_iota(jnp.int32, (1, cg), 1)
    wide = lax.broadcasted_iota(jnp.int32, (1, facts.shape[1]), 1)
    level_at = lax.broadcasted_iota(jnp.int32, (table.shape[0], 1), 0).astype(f32)
    for s in range(nz):
        clean, noise = blocks[s][:px].astype(f32), blocks[s][px : 2 * px].astype(f32)
        for p, x in enumerate((blocks[s][:px], blocks[s][px : 2 * px])):
            low[s, p] = x[:wid]
            high[s, p] = x[px - wid :]
        told = blocks[s][2 * px : 2 * px + 16].astype(f32)[:1]
        height, width, level = (
            jnp.sum(jnp.where(lane == c, told, 0.0), axis=1, keepdims=True) for c in range(3)
        )
        for which in range(2):
            at = which * nz + s
            hot = (level_at == level + which).astype(f32)
            fact = jnp.sum(hot * table[...], axis=0, keepdims=True)
            fact = jnp.where(wide == HEIGHT, height, jnp.where(wide == WIDTH, width, fact))
            facts[at : at + 1, :] = fact
            emb_row = jnp.sum(hot * emb_pair[...], axis=0, keepdims=True)
            emb[at : at + 1, :] = emb_row
            valid = valid_mask(fact, 0, row0[0], 0, (px, cg), hr, wid)
            n = jnp.maximum(jnp.sum(valid, axis=0, keepdims=True), 1.0)
            inner = spot(fact, 0, CIN) * (clean + spot(fact, 0, SIG) * noise) + emb_row
            mean = jnp.sum(valid * inner, axis=0, keepdims=True) / n
            off = inner - mean
            local[0, at : at + 1, :] = mean
            local[1, at : at + 1, :] = jnp.sum(valid * off * off, axis=0, keepdims=True)


def conv_kernel(nz, rows, hr, wid, starts, facts, emb, gain, shift, above, below, own_s, nbr_s, own_t, nbr_t, *refs):
    stats, blocks, refs = refs[:rows], refs[rows : rows + nz], refs[rows + nz :]
    parts, (ja, jb, m1a, m1b, m2a, m2b, ta, tb) = refs[: 2 * nz], refs[2 * nz :]
    cg = emb.shape[1]
    cd = cg // 2
    px = hr * wid
    tall = (hr + 2) * wid

    ci = lax.broadcasted_iota(jnp.int32, (cg, cg), 0) // GROUP_WIDTH
    cj = lax.broadcasted_iota(jnp.int32, (cg, cg), 1) // GROUP_WIDTH
    same = (ci == cj).astype(f32)
    height, width = facts[:, HEIGHT : HEIGHT + 1], facts[:, WIDTH : WIDTH + 1]
    whole = height * width * GROUP_WIDTH
    counts = [
        jnp.minimum(jnp.maximum(height - starts[n].astype(f32), 0.0), float(hr)) * width for n in range(rows)
    ]

    def group_mean(per_channel):
        return jnp.dot(per_channel, same, precision=lax.Precision.HIGHEST, preferred_element_type=f32) / whole

    mid = group_mean(sum(c * st[0] for c, st in zip(counts, stats)))
    squares = sum(st[1] + c * (st[0] - mid) * (st[0] - mid) for c, st in zip(counts, stats))
    dev = 1.0 / jnp.sqrt(group_mean(squares) + EPS)

    col = lax.broadcasted_iota(jnp.int32, (tall, cg), 0) % wid
    not_first = (col > 0).astype(f32)
    not_last = (col < wid - 1).astype(f32)

    def fan(value, kind):
        left = pltpu.roll(value, 1, 0) * not_first
        right = pltpu.roll(value, tall - 1, 0) * not_last
        return [
            jnp.concatenate([v[:, h * cd : (h + 1) * cd] for v in (left, value, right)], axis=1).astype(kind)
            for h in range(2)
        ]

    for s in range(nz):
        valid = valid_mask(facts, s, starts[0], -1, (tall, cg), hr, wid)
        clean, noise = [
            jnp.concatenate(
                [above[s, p].astype(f32), blocks[s][p * px : (p + 1) * px].astype(f32), below[s, p].astype(f32)], axis=0
            )
            for p in range(2)
        ]
        for which in range(2):
            at = which * nz + s
            inner = spot(facts, at, CIN) * (clean + spot(facts, at, SIG) * noise) + emb[at : at + 1, :]
            normed = (inner - mid[at : at + 1, :]) * dev[at : at + 1, :]
            preact = normed * gain[...] + shift[...]
            gate = 1.0 / (1.0 + jnp.exp(-preact))
            active = valid * (preact * gate)
            if which == 0:
                ta[s], tb[s] = fan(active, bf16)
            else:
                ja[s], jb[s] = fan(active, bf16)
                slope = valid * (gate * (1.0 + preact * (1.0 - gate)))
                m2a[s], m2b[s] = fan(slope, f32)
                m1a[s], m1b[s] = fan(slope * normed, f32)

    def conv(a, b, wa, wb):
        total = None
        for i in range(3):
            for j, w in ((a, wa), (b, wb)):
                left = j[:, i * wid : i * wid + px, :].reshape(nz * px, 3 * cd)
                term = jnp.dot(left, w[i], preferred_element_type=f32)
                total = term if total is None else total + term
        return total.reshape(nz, px, -1)

    student = conv(ja, jb, own_s, nbr_s)
    target = conv(ta, tb, own_t, nbr_t)
    half = px // 2
    for s in range(nz):
        part = spot(facts, nz + s, COUT) * student[s] - spot(facts, s, COUT) * target[s]
        parts[2 * s][...] = part[:half]
        parts[2 * s + 1][...] = part[half:]


def grad_out_kernel(nz, hr, wid, row0, facts, clean, noise, base_a, base_b, more_a, more_b, after, grad, loss):
    half = base_a.shape[0]
    count = spot(facts, 0, HEIGHT) * spot(facts, 0, WIDTH)
    total_loss = jnp.zeros((1, 1), f32)
    for n, (base, more) in enumerate(((base_a, more_a), (base_b, more_b))):
        span = slice(n * half, (n + 1) * half)
        x, e = clean[span].astype(f32), noise[span].astype(f32)
        terms = []
        for at in (nz, 0):
            noisy = x + spot(facts, at, SIG) * e
            terms.append(spot(facts, at, BYP) * noisy + spot(facts, at, COUT) * (spot(facts, at, CIN) * noisy))
        valid = valid_mask(facts, 0, row0[0], n * half // wid, x.shape, hr, wid)
        delta = valid * (terms[0] - terms[1] + (base[...] + more[...]))
        total_loss += jnp.sum(jnp.sum(delta * delta, axis=0, keepdims=True), axis=1, keepdims=True)
        grad[span] = ((2.0 * spot(facts, nz, COUT) / count) * delta).astype(bf16)
    loss[...] = jnp.broadcast_to(total_loss / count, loss.shape)


def sums_kernel(nz, wid, own, nbr, m1a, m1b, m2a, m2b, *refs):
    grads, out = refs[:nz], refs[nz]
    left = jnp.concatenate([g[...] for g in grads], axis=0)
    px = grads[0].shape[0]
    out[...] = jnp.zeros(out.shape, f32)
    for h, (w, m1, m2) in enumerate(((own, m1a, m2a), (nbr, m1b, m2b))):
        for i in range(3):
            seen = lax.dot_general(left, w[i], (((1,), (1,)), ((), ())), preferred_element_type=f32)
            for row, mm in enumerate((m1, m2)):
                field = mm[:, i * wid : i * wid + px, :].reshape(nz * px, -1)
                out[2 * h + row : 2 * h + row + 1, :] += jnp.sum(seen * field, axis=0, keepdims=True)


def grad_kernel(nz, wid, j, *refs):
    grads, out = refs[:nz], refs[-1]
    px = grads[0].shape[0]
    right = jnp.concatenate([g[...] for g in grads], axis=0)
    for i in range(3):
        left = j[:, i * wid : i * wid + px, :].reshape(nz * px, -1)
        out[i] = lax.dot_general(left, right, (((0,), (0,)), ((), ())), preferred_element_type=f32)


def grad_split_kernel(nz, wid, core, j, before, *refs):
    grads, (mine, other, total) = refs[:nz], refs[nz:]
    px = grads[0].shape[0]
    right = jnp.concatenate([g[...] for g in grads], axis=0)
    n = before.shape[1]
    for i in range(3):
        left = j[:, i * wid : i * wid + px, :].reshape(nz * px, -1)
        got = lax.dot_general(left, right, (((0,), (0,)), ((), ())), preferred_element_type=f32)
        total[i * n : (i + 1) * n, :] = before[i] + got
    half = mine.shape[0]
    mine[...] = total[pl.ds(pl.multiple_of(core[0] * half, 8), half), :]
    other[...] = total[pl.ds(pl.multiple_of((1 - core[0]) * half, 8), half), :]


def add_kernel(a, b, after, out):
    out[...] = a[...] + b[...]


def small_sum(value):
    rows, dp = lax.axis_size("rows"), lax.axis_size("dp")
    for axis, count, base in (("rows", rows, 1), ("dp", 2, 1), ("dp", dp // 2, 2)):
        every = lax.axis_size(axis)
        terms = [value] + [lax.ppermute(value, axis, xor_perm(every, s * base)) for s in range(1, count)]
        while len(terms) > 1:
            terms = [terms[n] + terms[n + 1] for n in range(0, len(terms), 2)]
        value = terms[0]
    return value


def shards(clean, noise, heights, widths, levels, gain, shift, emb_table, w_student, w_ema):
    dp, rows = lax.axis_size("dp"), lax.axis_size("rows")
    nz = dp // 2
    channels = clean.shape[3]
    hr, wid = clean.shape[1], clean.shape[2]
    px = hr * wid
    cd = channels // dp
    cg = 2 * cd
    tall = (hr + 2) * wid
    k = lax.axis_index("dp")
    r = lax.axis_index("rows")
    clean, noise = clean.reshape(px, channels), noise.reshape(px, channels)

    told = jnp.stack([heights[0], widths[0], levels[0], k.astype(jnp.int32)])
    blocks = call(
        functools.partial(payload_kernel, nz, cd),
        [sds((2 * px + 16, cg), bf16)] * nz,
        [told, clean, noise],
        {0: SMEM},
    )
    with jax.named_scope("a_send"):
        for s in range(nz - 1, 0, -1):
            blocks[s] = along_z(blocks[s], s)

    own_s = w_student.transpose(1, 2, 0, 3).reshape(9 * cd, channels)
    own_t = w_ema.transpose(1, 2, 0, 3).reshape(9 * cd, channels)
    nbr_s, nbr_t = swap_weights(own_s, own_t, blocks[0])
    own_s, own_t, nbr_s, nbr_t = (w.reshape(3, 3 * cd, channels) for w in (own_s, own_t, nbr_s, nbr_t))

    sigma = sigma_table()
    in_scale, bypass, out_scale = scale_factors(sigma)
    table = jnp.stack([sigma, in_scale, out_scale, bypass], 1)
    table = jnp.pad(table, ((0, 16 - NSTEPS), (0, 124)))
    pair_gain = jnp.concatenate([lax.dynamic_slice_in_dim(gain, (k ^ j) * cd, cd, 0) for j in range(2)])[None]
    pair_shift = jnp.concatenate([lax.dynamic_slice_in_dim(shift, (k ^ j) * cd, cd, 0) for j in range(2)])[None]
    pair_emb = jnp.concatenate([lax.dynamic_slice_in_dim(emb_table, (k ^ j) * cd, cd, 1) for j in range(2)], 1)
    pair_emb = jnp.pad(pair_emb, ((0, 16 - NSTEPS), (0, 0)))
    starts = jnp.stack([(r ^ s) * hr for s in range(rows)]).astype(jnp.int32)

    border = sds((nz, 2, wid, cg), bf16)
    facts, emb, local, low, high = call(
        functools.partial(stats_kernel, nz, hr, wid),
        [sds((2 * nz, 128), f32), sds((2 * nz, cg), f32), sds((2, 2 * nz, cg), f32), border, border],
        [starts[:1], table, pair_emb] + list(blocks),
        {0: SMEM},
    )
    with jax.named_scope("stat_send"):
        stats = [local] + [along_rows(local, s) for s in range(1, rows)]
    above, below = rows_halo(low, high)

    work = 2 * nz * px * 9 * cd * channels
    outs = [sds((px // 2, channels), f32)] * (2 * nz)
    outs += [sds((nz, tall, 3 * cd), bf16)] * 2 + [sds((nz, tall, 3 * cd), f32)] * 4
    res = call(
        functools.partial(conv_kernel, nz, rows, hr, wid),
        outs,
        [starts, facts, emb, pair_gain, pair_shift, above, below, own_s, nbr_s, own_t, nbr_t] + stats + list(blocks),
        {0: SMEM},
        flops=4 * work,
        scratch=[pltpu.VMEM((nz, tall, 3 * cd), bf16)] * 2,
    )
    part = [[res[2 * s], res[2 * s + 1]] for s in range(nz)]
    j_own, j_nbr, m1a, m1b, m2a, m2b = res[2 * nz :]

    bit = 1
    while bit < nz:
        for s in range(nz - 2 * bit, -1, -2 * bit):
            with jax.named_scope("d_send"):
                more = [along_z(part[s ^ bit][h], bit) for h in range(2)]
            if 2 * bit < nz:
                part[s] = [part[s][h] + more[h] for h in range(2)]
        bit *= 2
    with jax.named_scope("jx_send"):
        j_x = along_x(j_nbr)

    grad, loss_local = call(
        functools.partial(grad_out_kernel, nz, hr, wid),
        [sds((px, channels), bf16), sds((8, 128), f32)],
        [starts[:1], facts, clean, noise] + part[0] + more + [j_x],
        {0: SMEM, 8: ANY},
    )
    grads = {0: grad}
    bit = nz // 2
    while bit >= 1:
        for s in sorted(grads):
            with jax.named_scope("f_send"):
                grads[s ^ bit] = along_z(grads[s], bit)
        bit //= 2
    grad_z = [grads[s] for s in range(nz)]
    with jax.named_scope("fx_send"):
        grad_x = [along_x(g) for g in grad_z]

    (small,) = call(
        functools.partial(sums_kernel, nz, wid),
        [sds((8, 3 * cd), f32)],
        [own_s, nbr_s, m1a, m1b, m2a, m2b] + grad_z,
        flops=2 * work,
    )
    small = small[:4].reshape(2, 2, 3, cd).sum(2)
    placed = jnp.zeros((2, dp, cd), f32)
    for h in range(2):
        placed = lax.dynamic_update_slice(placed, small[h][:, None, :], (0, k ^ h, 0))
    flat = jnp.concatenate([placed.reshape(2 * channels), loss_local[0, :1]])
    flat = jnp.pad(flat, (0, -flat.shape[0] % 1024)).reshape(-1, 128)
    with jax.named_scope("small"):
        flat = small_sum(flat)

    (owned,) = call(
        functools.partial(grad_kernel, nz, wid), [sds((3, 3 * cd, channels), f32)], [j_own] + grad_z, flops=work
    )
    half = 9 * cd // 2
    core = (r & 1).astype(jnp.int32)
    if half % 8:
        (rest,) = call(
            functools.partial(grad_kernel, nz, wid), [sds((3, 3 * cd, channels), f32)], [j_x] + grad_x, flops=work
        )
        owned = (owned + rest).reshape(9 * cd, channels)
        mine = jnp.where(core == 0, owned[:half], owned[half:])
        other = jnp.where(core == 0, owned[half:], owned[:half])
    else:
        mine, other = call(
            functools.partial(grad_split_kernel, nz, wid),
            [sds((half, channels), f32)] * 2,
            [core[None], j_x, owned] + grad_x,
            {0: SMEM},
            flops=work,
            scratch=[pltpu.VMEM((9 * cd, channels), f32)],
        )
    with jax.named_scope("h_core"):
        came = along_rows(other, 1)
    mine = mine + came
    step = 2
    while step < rows:
        with jax.named_scope("h_y"):
            came = along_rows(mine, step)
        (mine,) = call(add_kernel, [sds(mine.shape, f32)], [mine, came, flat], {2: ANY})
        step *= 2
    with jax.named_scope("h_back"):
        back = along_rows(mine, 1)
    owned = jnp.concatenate([jnp.where(core == 0, mine, back), jnp.where(core == 0, back, mine)], 0)
    grad_conv = owned.reshape(3, 3, cd, channels).transpose(2, 0, 1, 3)
    flat = flat.reshape(-1)
    loss = flat[2 * channels] / (dp * channels)
    return grad_conv, flat[:channels], flat[channels : 2 * channels], loss


def solution(mesh):
    placed = (
        P("dp", "rows", None, None),
        P("dp", "rows", None, None),
        P("dp"),
        P("dp"),
        P("dp"),
        P(),
        P(),
        P(),
        P("dp", None, None, None),
        P("dp", None, None, None),
    )
    return jax.shard_map(
        shards,
        mesh=mesh,
        in_specs=placed,
        out_specs=(P("dp", None, None, None), P(), P(), P()),
        check_vma=False,
    )
```

```python
import functools

import jax
import jax.numpy as jnp
import numpy as np
from jax import lax
from jax.experimental import pallas as pl
from jax.experimental.pallas import tpu as pltpu
from jax.sharding import PartitionSpec as P


GROUP_WIDTH = 20
NSTEPS = 10
SIGMA_DATA = 0.5
SIGMA_FLOOR = 0.002
SIGMA_CEIL = 80.0
EPS = 1e-05

SIG, CIN, COUT, BYP, HEIGHT, WIDTH = range(6)


f32, bf16 = jnp.float32, jnp.bfloat16


def level_table():
    one = np.float32
    ladder = np.arange(NSTEPS, dtype=one) / one(NSTEPS - 1)
    lowest = SIGMA_FLOOR ** (1.0 / 7.0)
    highest = SIGMA_CEIL ** (1.0 / 7.0)
    sigma = (one(lowest) + ladder * one(highest - lowest)).astype(np.float64) ** 7
    sigma = sigma.astype(one)
    root = np.sqrt(sigma * sigma + one(SIGMA_DATA**2))
    lifted = sigma - one(SIGMA_FLOOR)
    table = np.zeros((16, 128), one)
    table[:NSTEPS, SIG] = sigma
    table[:NSTEPS, CIN] = one(1.0) / root
    table[:NSTEPS, COUT] = one(SIGMA_DATA) * lifted / root
    table[:NSTEPS, BYP] = one(SIGMA_DATA**2) / (lifted * lifted + one(SIGMA_DATA**2))
    return table


def xor_perm(count, step):
    return [(i, i ^ step) for i in range(count)]


def along_z(value, step):
    return lax.ppermute(value, "dp", xor_perm(lax.axis_size("dp"), 2 * step))


def along_x(value):
    return lax.ppermute(value, "dp", xor_perm(lax.axis_size("dp"), 1))


def along_rows(value, step):
    return lax.ppermute(value, "rows", xor_perm(lax.axis_size("rows"), step))


ANY = pl.BlockSpec(memory_space=pl.ANY)
HBM = pl.BlockSpec(memory_space=pltpu.HBM)
SMEM = pl.BlockSpec(memory_space=pltpu.SMEM)
VMEM = pl.BlockSpec(memory_space=pltpu.VMEM)
sds = jax.ShapeDtypeStruct


def call(kernel, outs, args, specs=None, flops=0, scratch=(), grant=24, to=None):
    specs = specs or {}
    moved = sum(a.size * a.dtype.itemsize for n, a in enumerate(args) if specs.get(n) not in (ANY, HBM))
    moved += sum(a.size * a.dtype.itemsize for a in outs)
    res = pl.pallas_call(
        kernel,
        out_shape=outs,
        in_specs=[specs.get(n, VMEM) for n in range(len(args))],
        out_specs=[to or VMEM] * len(outs),
        scratch_shapes=list(scratch),
        cost_estimate=pl.CostEstimate(flops=flops, bytes_accessed=moved, transcendentals=0),
        compiler_params=pltpu.CompilerParams(vmem_limit_bytes=grant << 20),
    )(*args)
    return list(res)


def picker(channels, cd, s):
    cg = 2 * cd
    k = lax.axis_index("dp")
    source = lax.broadcasted_iota(jnp.int32, (channels, cg), 0)
    at = lax.broadcasted_iota(jnp.int32, (channels, cg), 1)
    base = ((k // 2) ^ s) * cg
    own, nbr = base + (k % 2) * cd, base + (1 - k % 2) * cd
    return (source == jnp.where(at < cd, own + at, nbr + at - cd)).astype(f32)


def payload_kernel(nz, cd, heights, widths, levels, clean, noise, *outs):
    px, channels = clean.shape
    block = 2 * px // nz
    lane = lax.broadcasted_iota(jnp.int32, (8, channels), 1)
    row = jnp.where(lane == 0, heights[...], jnp.where(lane == 1, widths[...], jnp.where(lane == 2, levels[...], 0)))
    for s in range(nz - 1, -1, -1):
        pick = picker(channels, cd, s).astype(bf16)
        taken = jnp.concatenate(
            [jnp.dot(x[...], pick, preferred_element_type=f32) for x in (clean, noise)], axis=0
        )
        wide = jnp.concatenate([taken[q * block : (q + 1) * block] for q in range(nz)], axis=1)
        outs[s][...] = jnp.concatenate([wide, row.astype(f32)], axis=0).astype(bf16)


def pair_kernel(cd, emb, gain, shift, out):
    channels = emb.shape[1]
    rows = jnp.concatenate([emb[...], gain[...], shift[...], jnp.zeros((14 - NSTEPS, channels), f32)], axis=0)
    out[...] = jnp.dot(
        rows, picker(channels, cd, 0), precision=lax.Precision.HIGHEST, preferred_element_type=f32
    )


def spot(rows, at, column):
    return rows[at : at + 1, column : column + 1]


def valid_mask(facts, at, row0, first, shape, wid):
    pixel = lax.broadcasted_iota(jnp.int32, shape, 0)
    row = (pixel // wid + (first + row0)).astype(f32)
    col = (pixel % wid).astype(f32)
    return ((row >= 0) & (row < spot(facts, at, HEIGHT)) & (col < spot(facts, at, WIDTH))).astype(f32)


def near_steps(rows):
    return [step for step in range(1, rows) if step & (step + 1) == 0]


def stats_kernel(nz, rows, hr, wid, table, pair, *refs):
    packed, (facts, emb, cn, *outs) = refs[:nz], refs[nz:]
    px = hr * wid
    block = 2 * px // nz
    r = lax.axis_index("rows")
    cg = emb.shape[1]
    lane = lax.broadcasted_iota(jnp.int32, (1, cg), 1)
    wide = lax.broadcasted_iota(jnp.int32, (1, facts.shape[1]), 1)
    level_at = lax.broadcasted_iota(jnp.int32, (table.shape[0], 1), 0).astype(f32)
    sums = [[], [], [], []]
    low, high = [], []
    for s in range(nz):
        whole = packed[s][...].astype(f32)
        flat = jnp.concatenate([whole[:block, q * cg : (q + 1) * cg] for q in range(nz)], axis=0)
        clean, noise = flat[:px], flat[px:]
        cn[s, 0] = clean.astype(bf16)
        cn[s, 1] = noise.astype(bf16)
        low.append(jnp.concatenate([clean[:wid], noise[:wid]], axis=0))
        high.append(jnp.concatenate([clean[px - wid :], noise[px - wid :]], axis=0))
        told = whole[block : block + 1, :cg]
        height, width, level = (
            jnp.sum(jnp.where(lane == c, told, 0.0), axis=1, keepdims=True) for c in range(3)
        )
        for which in range(2):
            at = which * nz + s
            hot = (level_at == level + which).astype(f32)
            fact = jnp.sum(hot * table[...], axis=0, keepdims=True)
            fact = jnp.where(wide == HEIGHT, height, jnp.where(wide == WIDTH, width, fact))
            facts[at : at + 1, :] = fact
            emb_row = jnp.sum(hot * pair[...], axis=0, keepdims=True)
            emb[at : at + 1, :] = emb_row
            valid = valid_mask(fact, 0, r * hr, 0, (px, cg), wid)
            n = jnp.maximum(jnp.sum(valid, axis=0, keepdims=True), 1.0)
            inner = spot(fact, 0, CIN) * (clean + spot(fact, 0, SIG) * noise) + emb_row
            mean = jnp.sum(valid * inner, axis=0, keepdims=True) / n
            off = inner - mean
            sums[which].append(mean)
            sums[2 + which].append(jnp.sum(valid * off * off, axis=0, keepdims=True))
    local = [jnp.concatenate(row, axis=1) for row in sums]
    local = jnp.concatenate(local + [jnp.zeros((4, nz * cg), f32)], axis=0)
    low, high = jnp.concatenate(low, axis=1), jnp.concatenate(high, axis=1)
    outs[0][...] = local
    for n, step in enumerate(near_steps(rows)):
        outs[1 + n][:8] = local
        outs[1 + n][8:] = jnp.where((r ^ step) > r, high, low)


def fan(value, kind, wid, cd):
    tall = value.shape[0]
    col = lax.broadcasted_iota(jnp.int32, value.shape, 0) % wid
    left = pltpu.roll(value, 1, 0) * (col > 0).astype(f32)
    right = pltpu.roll(value, tall - 1, 0) * (col < wid - 1).astype(f32)
    taps = [v.astype(kind) for v in (left, value, right)]
    return [jnp.concatenate([v[:, h * cd : (h + 1) * cd] for v in taps], axis=1) for h in range(2)]


def borders(near):
    r = lax.axis_index("rows")
    above = below = None
    for step, message in near.items():
        rows = message[8:]
        above = rows if above is None else jnp.where((r ^ step) == r - 1, rows, above)
        below = rows if below is None else jnp.where((r ^ step) == r + 1, rows, below)
    return above, below


def pre_activation(cn, above, below, facts, emb, mid, dev, pair, nz, s, which):
    cg = emb.shape[1]
    wid = above.shape[0] // 2
    clean, noise = [
        jnp.concatenate(
            [
                above[p * wid : (p + 1) * wid, s * cg : (s + 1) * cg],
                cn[s, p].astype(f32),
                below[p * wid : (p + 1) * wid, s * cg : (s + 1) * cg],
            ],
            axis=0,
        )
        for p in range(2)
    ]
    at = which * nz + s
    inner = spot(facts, at, CIN) * (clean + spot(facts, at, SIG) * noise) + emb[at : at + 1, :]
    normed = (inner - mid[at : at + 1, :]) * dev[at : at + 1, :]
    return normed, normed * pair[NSTEPS : NSTEPS + 1, :] + pair[NSTEPS + 1 : NSTEPS + 2, :]


def act_kernel(nz, rows, hr, wid, facts, emb, pair, cn, *refs):
    messages, (left_own, left_nbr, ja, jb, mid_out, dev_out) = refs[:rows], refs[rows:]
    r = lax.axis_index("rows")
    cg = emb.shape[1]
    cd = cg // 2
    px = hr * wid
    tall = (hr + 2) * wid

    ci = lax.broadcasted_iota(jnp.int32, (cg, cg), 0) // GROUP_WIDTH
    cj = lax.broadcasted_iota(jnp.int32, (cg, cg), 1) // GROUP_WIDTH
    same = (ci == cj).astype(f32)
    height, width = facts[:, HEIGHT : HEIGHT + 1], facts[:, WIDTH : WIDTH + 1]
    whole = height * width * GROUP_WIDTH
    counts = [
        jnp.minimum(jnp.maximum(height - ((r ^ n) * hr).astype(f32), 0.0), float(hr)) * width for n in range(rows)
    ]
    stats = []
    for message in messages:
        told = message[:8]
        stats.append(
            [
                jnp.concatenate(
                    [told[q + w : q + w + 1, s * cg : (s + 1) * cg] for w in range(2) for s in range(nz)], axis=0
                )
                for q in (0, 2)
            ]
        )

    def group_mean(per_channel):
        return jnp.dot(per_channel, same, precision=lax.Precision.HIGHEST, preferred_element_type=f32) / whole

    mid = group_mean(sum(c * st[0] for c, st in zip(counts, stats)))
    squares = sum(st[1] + c * (st[0] - mid) * (st[0] - mid) for c, st in zip(counts, stats))
    dev = 1.0 / jnp.sqrt(group_mean(squares) + EPS)
    mid_out[...] = mid
    dev_out[...] = dev

    above, below = borders({step: messages[step] for step in near_steps(rows)})
    for s in range(nz):
        valid = valid_mask(facts, s, r * hr, -1, (tall, cg), wid)
        for which in range(2):
            _, preact = pre_activation(cn, above, below, facts, emb, mid, dev, pair, nz, s, which)
            active = valid * (preact * (1.0 / (1.0 + jnp.exp(-preact))))
            halves = fan(active, bf16, wid, cd)
            if which == 1:
                ja[s], jb[s] = halves
            for left, side in zip((left_own, left_nbr), halves):
                for i in range(3):
                    left[which, s * px : (s + 1) * px, 3 * i * cd : 3 * (i + 1) * cd] = side[i * wid : i * wid + px]


def by_core(first, second, work):
    core = lax.axis_index("rows") % 2

    @pl.when(core == 0)
    def _():
        work(first, second)

    @pl.when(core == 1)
    def _():
        work(second, first)


TOP = 32767.0
FINE = 256.0


def row_units(codes):
    return jnp.exp(codes * (float(np.log(2.0)) / FINE)) * (1.0 / TOP)


def encode_rows(value, out):
    n, o = value.shape
    peak = jnp.maximum(jnp.max(jnp.abs(value), axis=1, keepdims=True), 1e-30)
    codes = jnp.ceil(jnp.log(peak) * (FINE / float(np.log(2.0))))
    whole = jnp.clip(jnp.round(value / row_units(codes)), -TOP, TOP)
    out[:n] = whole.astype(jnp.int32).astype(jnp.int16)
    across = jnp.broadcast_to(codes, (n, 128)).T[:8]
    out[n:] = jnp.concatenate([across, jnp.zeros((8, o - n), f32)], axis=1).astype(jnp.int32).astype(jnp.int16)


def decode_rows(ref):
    n = ref.shape[0] - 8
    codes = ref[n:].astype(jnp.int32).astype(f32)[:1, :n]
    units = row_units(jnp.broadcast_to(codes, (128, n)).T[:, :1])
    return ref[:n].astype(jnp.int32).astype(f32) * units


def conv_kernel(nz, px, facts, left_own, left_nbr, own_s, own_t, first, second, base, *coded):
    def work(nbr_s, nbr_t):
        def conv(which, own, nbr):
            near = jnp.dot(left_own[which], own[...], preferred_element_type=f32)
            return near + jnp.dot(left_nbr[which], nbr[...], preferred_element_type=f32)

        student, target = conv(1, own_s, nbr_s), conv(0, own_t, nbr_t)
        for s in range(nz - 1, -1, -1):
            span = slice(s * px, (s + 1) * px)
            part = spot(facts, nz + s, COUT) * student[span] - spot(facts, s, COUT) * target[span]
            if s:
                encode_rows(part, coded[s - 1])
            else:
                base[...] = part

    by_core(first, second, work)


def slope_kernel(nz, rows, hr, wid, facts, emb, pair, cn, mid, dev, *refs):
    steps = near_steps(rows)
    above, below = borders(dict(zip(steps, refs)))
    m1a, m1b, m2a, m2b = refs[len(steps) :]
    r = lax.axis_index("rows")
    cg = emb.shape[1]
    for s in range(nz):
        valid = valid_mask(facts, s, r * hr, -1, ((hr + 2) * wid, cg), wid)
        normed, preact = pre_activation(cn, above, below, facts, emb, mid, dev, pair, nz, s, 1)
        gate = 1.0 / (1.0 + jnp.exp(-preact))
        slope = valid * (gate * (1.0 + preact * (1.0 - gate)))
        m2a[s], m2b[s] = fan(slope, f32, wid, cg // 2)
        m1a[s], m1b[s] = fan(slope * normed, f32, wid, cg // 2)


def grad_out_kernel(nz, hr, wid, facts, clean, noise, base, *refs):
    coded, (_, _, grad, *halves, loss) = refs[: nz - 1], refs[nz - 1 :]
    count = spot(facts, 0, HEIGHT) * spot(facts, 0, WIDTH)
    x, e = clean[...].astype(f32), noise[...].astype(f32)
    terms = []
    for at in (nz, 0):
        noisy = x + spot(facts, at, SIG) * e
        terms.append(spot(facts, at, BYP) * noisy + spot(facts, at, COUT) * (spot(facts, at, CIN) * noisy))
    total = base[...]
    for ref in coded:
        total = total + decode_rows(ref)
    valid = valid_mask(facts, 0, lax.axis_index("rows") * hr, 0, x.shape, wid)
    delta = valid * (terms[0] - terms[1] + total)
    rounded = ((2.0 * spot(facts, nz, COUT) / count) * delta).astype(bf16)
    grad[...] = rounded
    for n, half in enumerate(halves):
        half[...] = rounded[n * half.shape[0] : (n + 1) * half.shape[0]]
    squares = jnp.sum(jnp.sum(delta * delta, axis=0, keepdims=True), axis=1, keepdims=True)
    loss[...] = jnp.broadcast_to(squares / count, loss.shape)


def sums_kernel(nz, wid, cd, loss, own, first, second, m1a, m1b, m2a, m2b, *refs):
    grads, (out, sums) = refs[:-2], refs[-2:]
    left = jnp.concatenate([g[...] for g in grads], axis=0)
    px = left.shape[0] // nz
    channels = out.shape[1]
    k = lax.axis_index("dp")

    def work(nbr, _):
        for h, (w, m1, m2) in enumerate(((own, m1a, m2a), (nbr, m1b, m2b))):
            total = [None, None]
            for i in range(3):
                taps = w[3 * i * cd : 3 * (i + 1) * cd, :]
                seen = lax.dot_general(left, taps, (((1,), (1,)), ((), ())), preferred_element_type=f32)
                for row, mm in enumerate((m1, m2)):
                    field = mm[:, i * wid : i * wid + px, :].reshape(nz * px, -1)
                    term = jnp.sum(seen * field, axis=0, keepdims=True)
                    total[row] = term if i == 0 else total[row] + term
            for row in range(2):
                at = 8 * h + row
                sums[at : at + 1, :] = sum(total[row][:, j * cd : (j + 1) * cd] for j in range(3))
            sums[8 * h + 2 : 8 * (h + 1), :] = jnp.zeros((6, cd), f32)

    by_core(first, second, work)
    source = lax.broadcasted_iota(jnp.int32, (cd, channels), 0)
    at = lax.broadcasted_iota(jnp.int32, (cd, channels), 1)
    placed = jnp.zeros((8, channels), f32)
    for h in range(2):
        spread = (at == source + (k ^ h) * cd).astype(f32)
        placed += jnp.dot(sums[8 * h : 8 * (h + 1), :], spread, precision=lax.Precision.HIGHEST, preferred_element_type=f32)
    row = lax.broadcasted_iota(jnp.int32, (8, channels), 0)
    out[...] = jnp.where(row == 2, loss[:1, :1], placed)


def grad_kernel(nz, wid, after, j, *refs):
    grads, out = refs[:-1], refs[-1]
    right = jnp.concatenate([g[...] for g in grads], axis=0)
    px = right.shape[0] // nz
    for i in range(3):
        left = j[:, i * wid : i * wid + px, :].reshape(nz * px, -1)
        got = lax.dot_general(left, right, (((0,), (0,)), ((), ())), preferred_element_type=f32)
        out[i] = got[: out.shape[1]]


def grad_split_kernel(nz, wid, j, before, *refs):
    grads, (mine, other, total) = refs[:-3], refs[-3:]
    core = lax.axis_index("rows") % 2
    right = jnp.concatenate([g[...] for g in grads], axis=0)
    px = right.shape[0] // nz
    n = before.shape[1]
    for i in range(3):
        left = j[:, i * wid : i * wid + px, :].reshape(nz * px, -1)
        got = lax.dot_general(left, right, (((0,), (0,)), ((), ())), preferred_element_type=f32)
        total[i * n : (i + 1) * n, :] = before[i] + got[:n]
    half = mine.shape[0]
    mine[...] = total[pl.ds(pl.multiple_of(core * half, 8), half), :]
    other[...] = total[pl.ds(pl.multiple_of((1 - core) * half, 8), half), :]


def pieces_of(rows, unit):
    count = next((c for c in (6, 5, 4, 3, 2) if rows % (c * unit) == 0), 1)
    size = rows // count
    return [(n * size, size) for n in range(count)]


def choose_kernel(own_s, own_t, out, held, sems):
    core = lax.axis_index("rows") % 2
    spans = pieces_of(own_s.shape[0], 16)

    def loads(own):
        return [
            pltpu.make_async_copy(own.at[pl.ds(at, size), :], held.at[pl.ds(at, size), :], sems.at[0, n])
            for n, (at, size) in enumerate(spans)
        ]

    for n, own in enumerate((own_s, own_t)):

        @pl.when(core == n)
        def _():
            for load in loads(own):
                load.start()

    stores = [
        pltpu.make_async_copy(held.at[pl.ds(at, size), :], out.at[pl.ds(at, size), :], sems.at[1, n])
        for n, (at, size) in enumerate(spans)
    ]
    for load, store in zip(loads(own_s), stores):
        load.wait()
        store.start()
    for store in stores:
        store.wait()


def join_kernel(mine, back, out, sems):
    half = mine.shape[0]
    core = lax.axis_index("rows") % 2
    copies = [
        pltpu.make_async_copy(
            part.at[pl.ds(at, size), :], out.at[pl.ds(pl.multiple_of(side * half + at, 8), size), :], sems.at[h, n]
        )
        for h, (part, side) in enumerate(((mine, core), (back, 1 - core)))
        for n, (at, size) in enumerate(pieces_of(half, 8))
    ]
    for copy in copies:
        copy.start()
    for copy in copies:
        copy.wait()


def code_kernel(a, b, after, code, scale):
    value = a[...] + b[...]
    n = value.shape[0]
    peak = jnp.max(jnp.abs(value), axis=1, keepdims=True)
    up = jnp.where(peak > 0.0, TOP / jnp.where(peak > 0.0, peak, 1.0), 0.0)
    code[...] = jnp.round(value * up).astype(jnp.int32).astype(jnp.int16)
    units = jnp.concatenate([peak / TOP, jnp.zeros((scale.shape[1] - n, 1), f32)], axis=0)
    scale[...] = jnp.broadcast_to(units, (scale.shape[1], 128)).T[:8]


def decode_kernel(code_a, scale_a, code_b, scale_b, *refs):
    out = refs[-1]
    n = out.shape[0]
    terms = []
    for code, scale in ((code_a, scale_a), (code_b, scale_b)):
        units = jnp.broadcast_to(scale[:1, :], (128, scale.shape[1])).T[:n, :1]
        terms.append(code[...].astype(jnp.int32).astype(f32) * units)
    out[...] = terms[0] + terms[1]


def small_sum(value, axis, count, base):
    every = lax.axis_size(axis)
    terms = [value] + [lax.ppermute(value, axis, xor_perm(every, s * base)) for s in range(1, count)]
    while len(terms) > 1:
        terms = [terms[n] + terms[n + 1] for n in range(0, len(terms), 2)]
    return terms[0]


def step(clean, noise, heights, widths, levels, gain, shift, emb_table, w_student, w_ema):
    dp, rows = lax.axis_size("dp"), lax.axis_size("rows")
    nz = dp // 2
    channels = clean.shape[3]
    hr, wid = clean.shape[1], clean.shape[2]
    px = hr * wid
    cd = channels // dp
    cg = 2 * cd
    tall = (hr + 2) * wid
    core = lax.axis_index("rows") % 2
    clean, noise = clean.reshape(px, channels), noise.reshape(px, channels)

    own_s = w_student.transpose(1, 2, 0, 3).reshape(9 * cd, channels)
    own_t = w_ema.transpose(1, 2, 0, 3).reshape(9 * cd, channels)
    (chosen,) = call(
        choose_kernel, [sds(own_s.shape, bf16)], [own_s, own_t], {0: HBM, 1: HBM},
        scratch=[pltpu.VMEM(own_s.shape, bf16), pltpu.SemaphoreType.DMA((2, 6))], grant=60, to=HBM,
    )
    first = along_x(chosen)
    second = along_rows(first, 1)

    blocks = call(
        functools.partial(payload_kernel, nz, cd),
        [sds((2 * px // nz + 8, channels), bf16)] * nz,
        [heights.reshape(1, 1), widths.reshape(1, 1), levels.reshape(1, 1), clean, noise],
    )
    for s in range(nz - 1, 0, -1):
        blocks[s] = along_z(blocks[s], s)

    (pair,) = call(
        functools.partial(pair_kernel, cd), [sds((16, cg), f32)], [emb_table, gain[None], shift[None]]
    )
    steps = near_steps(rows)
    facts, emb, cn, local, *near = call(
        functools.partial(stats_kernel, nz, rows, hr, wid),
        [sds((2 * nz, 128), f32), sds((2 * nz, cg), f32), sds((nz, 2, px, cg), bf16), sds((8, channels), f32)]
        + [sds((8 + 2 * wid, channels), f32)] * len(steps),
        [jnp.asarray(level_table()), pair] + blocks,
    )
    messages = {0: local}
    for step in sorted(range(1, rows), reverse=True):
        messages[step] = along_rows(near[steps.index(step)] if step in steps else local, step)

    work = 2 * nz * px * 9 * cd * channels
    side = 3 * cd
    features = [facts, emb, pair, cn]
    left_own, left_nbr, j_own, j_nbr, mid, dev = call(
        functools.partial(act_kernel, nz, rows, hr, wid),
        [sds((2, nz * px, 9 * cd), bf16)] * 2 + [sds((nz, tall, side), bf16)] * 2 + [sds((2 * nz, cg), f32)] * 2,
        features + [messages[n] for n in range(rows)],
    )
    base, *coded = call(
        functools.partial(conv_kernel, nz, px),
        [sds((px, channels), f32)] + [sds((px + 8, channels), jnp.int16)] * (nz - 1),
        [facts, left_own, left_nbr, own_s, own_t, first, second],
        flops=4 * work,
        grant=32,
    )

    for s in range(nz - 1, 0, -1):
        coded[s - 1] = along_z(coded[s - 1], s)
    j_x = along_x(j_nbr)
    slopes = call(
        functools.partial(slope_kernel, nz, rows, hr, wid),
        [sds((nz, tall, side), f32)] * 4,
        features + [mid, dev] + [messages[n] for n in steps],
    )

    grad, *halves, loss = call(
        functools.partial(grad_out_kernel, nz, hr, wid),
        [sds((px, channels), bf16)] + [sds((px // 2, channels), bf16)] * 2 + [sds((8, 128), f32)],
        [facts, clean, noise, base] + coded + [j_x, slopes[0]],
        {nz + 3: ANY, nz + 4: ANY},
    )
    pieces = {0: [grad]}
    pieces_x = {0: [along_x(grad)]}
    bit = nz // 2
    while bit >= 1:
        for s in sorted(pieces):
            if s:
                pieces[s ^ bit] = [along_z(piece, bit) for piece in pieces[s]]
            elif bit == nz // 2:
                pieces[bit] = [along_z(piece, bit) for piece in halves]
            else:
                pieces[bit] = [along_z(grad, bit)]
        bit //= 2
    for s in range(1, nz):
        pieces_x[s] = [along_x(piece) for piece in pieces[s]]
    grad_z = [piece for s in range(nz) for piece in pieces[s]]
    grad_x = [piece for s in range(nz) for piece in pieces_x[s]]

    (small,) = call(
        functools.partial(sums_kernel, nz, wid, cd),
        [sds((8, channels), f32)],
        [loss, own_s, first, second] + slopes + grad_z,
        flops=2 * work,
        scratch=[pltpu.VMEM((16, cd), f32)],
    )
    summed = small_sum(small, "rows", rows, 1)

    shape = sds((3, 3 * cd, channels), f32)
    (owned,) = call(
        functools.partial(grad_kernel, nz, wid), [shape], [small, j_own] + grad_z, {0: ANY}, flops=work
    )
    half = 9 * cd // 2
    aligned = half % 8 == 0
    if aligned:
        mine, other = call(
            functools.partial(grad_split_kernel, nz, wid),
            [sds((half, channels), f32)] * 2,
            [j_x, owned] + grad_x,
            flops=work,
            scratch=[pltpu.VMEM((9 * cd, channels), f32)],
        )
    else:
        (rest,) = call(
            functools.partial(grad_kernel, nz, wid), [shape], [small, j_x] + grad_x, {0: ANY}, flops=work
        )
        owned = (owned + rest).reshape(9 * cd, channels)
        mine = jnp.where(core == 0, owned[:half], owned[half:])
        other = jnp.where(core == 0, owned[half:], owned[:half])
    came = along_rows(other, 1)
    every = small_sum(summed, "dp", 2, 1)
    every = small_sum(every, "dp", nz, 2)
    results = (every[0], every[1], every[2, 0] / (dp * channels))
    step = 2
    while step < rows:
        if aligned:
            coded, scale = call(
                code_kernel,
                [sds(mine.shape, jnp.int16), sds((8, -(-half // 128) * 128), f32)],
                [mine, came, summed],
                {2: ANY},
            )
            scale_y = along_rows(scale, step)
            coded_y = along_rows(coded, step)
            (mine,) = call(
                decode_kernel,
                [sds(mine.shape, f32)],
                [coded, scale, coded_y, scale_y, every],
                {4: ANY},
            )
        else:
            mine = mine + came
            mine = mine + along_rows(mine, step)
        came = jnp.zeros_like(mine)
        step *= 2
    back = along_rows(mine, 1)
    if aligned:
        (owned,) = call(
            join_kernel, [sds((2 * half, channels), f32)], [mine, back], scratch=[pltpu.SemaphoreType.DMA((2, 6))], to=ANY
        )
    else:
        owned = jnp.concatenate([jnp.where(core == 0, mine, back), jnp.where(core == 0, back, mine)], 0)
    grad_conv = owned.reshape(3, 3, cd, channels).transpose(2, 0, 1, 3)
    return (grad_conv,) + results


def solution(mesh):
    placed = (
        P("dp", "rows", None, None),
        P("dp", "rows", None, None),
        P("dp"),
        P("dp"),
        P("dp"),
        P(),
        P(),
        P(),
        P("dp", None, None, None),
        P("dp", None, None, None),
    )
    return jax.shard_map(
        step,
        mesh=mesh,
        in_specs=placed,
        out_specs=(P("dp", None, None, None), P(), P(), P()),
        check_vma=False,
    )
```
